32 devices in a mesh: grp: 8 (over y, x, core), seq: 4 (over z).
Axes of the slice: x: 2, y: 2, z: 4, core: 2. Of those that a mesh axis runs over, the one named last changes fastest.
Arguments:
- tokens: bfloat16 [8192, 512], P(('grp', 'seq')), parts along dimension 0, may hold values from -6 to 6
- group_pos: int32 [2048], P('grp'), parts along dimension 0, may hold values from 0 to 1023, as said below
- log_decay: float32 [8192, 16], P(('grp', 'seq')), parts along dimension 0, may hold values from -1 to 0, as said below
- in_weight: bfloat16 [512, 2176], replicated, may hold values from -0.25 to 0.25
- norm_gain: float32 [1024], replicated, may hold values from 0.1 to 1.9
- out_weight: bfloat16 [1024, 512], replicated, may hold values from -0.1875 to 0.1875
- inner_gain: float32 [512], replicated, may hold values from 0.1 to 1.9
- qkv_weight: bfloat16 [4, 512, 192], P('seq'), may hold values from -1 to 1
- attn_out: bfloat16 [4, 64, 512], P('seq'), may hold values from -0.375 to 0.375
Outputs:
- result: bfloat16 [8192, 512], P(('grp', 'seq')), parts along dimension 0
The draws below stay inside these ranges and needn't reach their ends.
There are 8 independent parts, one for each index of `grp`. The reference program is written for one: setup_inputs(seed, part) draws one part's arguments, and reference() takes and returns one part's arrays. A program takes and returns all parts, laid end to end along the dimension named above; an argument that names none is the same for every part. Nothing has to cross between parts.
Inputs may be any that keep to these rules, and one draw needn't show every extreme that they name: `group_pos`: strictly increasing. Each device's 256 positions hold at least one group start and at most 128; some device holds exactly 128. `log_decay`: negative at every position.
All inputs are finite; a program needn't handle non-finite values.
Results may differ from the reference program's by a relative error of at most 0.0061.
Values may be sent and summed in bfloat16 or wider, within the bound.
No kernel may reach another device: no remote copies, remote signals or barrier semaphores. Data moves between devices by JAX's collectives and lax.ppermute only.
A program may use at most 64 MiB of HBM per device.

```python
import jax
import jax.numpy as jnp
from jax import lax

D = 512
E = 1024
HEADS = 16
HDIM = 64
NSTATE = 64
IHDIM = 64
TOK_DEV = 256
IHEADS = 4
IDIM = 256
SPAN_EXTENT = 1024
CH_DEV = 64
MOST = 128
NCH = 256
N_SEQ = 4


def draw_group_pos(key, part):
    first, second, third = jax.random.split(jax.random.fold_in(key, 11), 3)
    heavy = jax.random.randint(first, (), 0, N_SEQ)
    devices = jnp.arange(N_SEQ, dtype=jnp.int32)
    weights = jax.random.randint(second, (N_SEQ,), 1, 9)
    weights = jnp.where(devices == heavy, 0, weights)
    total_w = jnp.sum(weights)
    cuts = CH_DEV * weights // total_w
    remain = CH_DEV - jnp.sum(cuts)
    ranked = jnp.cumsum((weights > 0).astype(jnp.int32)) - 1
    extra = ((weights > 0) & (ranked < remain)).astype(jnp.int32)
    counts = jnp.where(devices == heavy, MOST, CH_DEV - cuts - extra)
    scores = jax.random.randint(third, (N_SEQ, TOK_DEV), 0, 2 ** 20) * TOK_DEV + jnp.arange(TOK_DEV, dtype=jnp.int32)[None, :]
    order = jnp.argsort(scores, axis=1)
    ranks = jnp.argsort(order, axis=1)
    chosen = ranks < counts[:, None]
    return jnp.nonzero(chosen.reshape(-1), size=NCH)[0].astype(jnp.int32)


def draw_log_decay(key, part):
    kf, kr, kq, kp, lookup_segment, lookup_segment_alias, kblk = jax.random.split(jax.random.fold_in(key, 17), 7)
    fast_share = 0.5
    fast = jax.random.uniform(kf, (HEADS,)) < fast_share
    slow_rate = jax.random.uniform(kr, (HEADS,), jnp.float32, 0.1, 0.35) / SPAN_EXTENT
    fast_rate = jax.random.uniform(kq, (HEADS,), jnp.float32, 1.0 / 50.0, 1.0 / 30.0)
    fading_factor = jnp.where(fast, fast_rate, slow_rate)
    approximate_estimate = jax.random.uniform(kp, (SPAN_EXTENT, HEADS), jnp.float32, 0.5, 1.5)
    segment_sequence = jnp.exp(jax.random.uniform(kblk, (N_SEQ, 1, HEADS), jnp.float32, -0.69, 0.69))
    segment_sequence = jnp.broadcast_to(segment_sequence, (N_SEQ, TOK_DEV, HEADS)).reshape(SPAN_EXTENT, HEADS)
    spike_locations = jax.random.randint(lookup_segment, (2,), 0, SPAN_EXTENT)
    spike_magnitude = jax.random.uniform(lookup_segment_alias, (2,), jnp.float32, 0.22, 0.51)
    spike_indicator = jnp.sum((jnp.arange(SPAN_EXTENT)[:, None] == spike_locations[None, :]).astype(jnp.float32) * spike_magnitude[None, :], axis=1)
    return -(fading_factor[None, :] * approximate_estimate * segment_sequence) - spike_indicator[:, None]


def draw_qkv_weight(key, part):
    first = jax.random.fold_in(jax.random.fold_in(key, 23), 0)
    base = jax.random.normal(first, (IHEADS, D, 3 * IHDIM), jnp.float32) * D ** (-0.5)
    return jnp.clip(base, -1.0, 1.0).astype(jnp.bfloat16)


def block_scale(stream_key, extent, shards, smallest, top_value):
    factor_of = 1.0
    for axis_at, parts in shards:
        draws = jax.random.uniform(jax.random.fold_in(jax.random.fold_in(stream_key, 6), axis_at), (parts,), jnp.float32, smallest / len(shards), top_value / len(shards))
        factor_of = factor_of * jnp.repeat(jnp.exp(draws), extent[axis_at] // parts).reshape((-1,) + (1,) * (len(extent) - 1 - axis_at))
    return factor_of


def normal_values(stream_key, shape, scale, reach, cuts=(), kind=jnp.bfloat16):
    loudness = block_scale(stream_key, shape, cuts, -0.22, 0.18) if cuts else 1.0
    drawn = jax.random.normal(stream_key, shape, jnp.float32) * scale * loudness
    return jnp.minimum(jnp.maximum(drawn, -reach), reach).astype(kind)


def setup_inputs(seed: int = 0, part: int = 0) -> dict:
    seeds = jax.random.split(jax.random.key(seed), 10)
    part_keys = jax.random.split(jax.random.fold_in(seeds[9], part), 10)
    return {
        "tokens": normal_values(part_keys[0], (SPAN_EXTENT, D), 1.0, 6.0, ((0, 4),)),
        "group_pos": draw_group_pos(jax.random.fold_in(jax.random.fold_in(seeds[9], part), 71), part),
        "log_decay": draw_log_decay(jax.random.fold_in(jax.random.fold_in(seeds[9], part), 71), part),
        "in_weight": normal_values(seeds[3], (D, 2 * E + 2 * NSTATE), D ** -0.5, 0.25),
        "norm_gain": jnp.clip(1.0 + 0.18 * jax.random.normal(seeds[4], (E,), jnp.float32), 0.1, 1.9),
        "out_weight": normal_values(seeds[5], (E, D), E ** -0.5, 0.1875),
        "inner_gain": jnp.clip(1.0 + 0.18 * jax.random.normal(seeds[6], (D,), jnp.float32), 0.1, 1.9),
        "qkv_weight": draw_qkv_weight(jax.random.fold_in(seeds[9], 71), part),
        "attn_out": normal_values(seeds[8], (IHEADS, IHDIM, D), IDIM ** -0.5, 0.375, ((0, 4),)),
    }


def rms_norm(values, gain):
    return values * lax.rsqrt(lax.optimization_barrier(jnp.mean(values * values, axis=-1, keepdims=True)) + 1e-05) * gain

def reference(tokens, group_pos, log_decay, in_weight, norm_gain, out_weight, inner_gain, qkv_weight, attn_out):
    proj = jnp.dot(tokens, in_weight, preferred_element_type=jnp.float32).astype(jnp.bfloat16)
    xs = proj[:, :E].astype(jnp.float32).reshape(SPAN_EXTENT, HEADS, HDIM)
    gate = proj[:, E:2 * E].astype(jnp.float32)
    bmat = proj[:, 2 * E:2 * E + NSTATE].astype(jnp.float32)
    cmat = proj[:, 2 * E + NSTATE:].astype(jnp.float32)

    def advance(state, inputs):
        decay, xrow, brow, crow = inputs
        state = jnp.exp(decay)[:, None, None] * state + xrow[:, :, None] * brow[None, None, :]
        out = jnp.einsum('hpn,n->hp', state, crow, precision=lax.Precision.HIGHEST)
        return (state, out)
    start = jnp.zeros((HEADS, HDIM, NSTATE), jnp.float32)
    _, ys = lax.scan(advance, start, (log_decay, xs, bmat, cmat))
    gated = ys.reshape(SPAN_EXTENT, E) * jax.nn.silu(gate)
    normed = rms_norm(gated, norm_gain).astype(jnp.bfloat16)
    hidden = (tokens.astype(jnp.float32) + jnp.dot(normed, out_weight, preferred_element_type=jnp.float32)).astype(jnp.bfloat16)
    rows = hidden[group_pos].astype(jnp.float32)
    rows_n = rms_norm(rows, inner_gain).astype(jnp.bfloat16)
    causal = jnp.arange(NCH)[:, None] >= jnp.arange(NCH)[None, :]

    def one_head(total, weights):
        w_qkv, w_out = weights
        qkv = jnp.dot(rows_n, w_qkv, preferred_element_type=jnp.float32).astype(jnp.bfloat16)
        query = qkv[:, :IHDIM]
        keys = qkv[:, IHDIM:2 * IHDIM]
        values = qkv[:, 2 * IHDIM:]
        scores = jnp.dot(query, keys.T, preferred_element_type=jnp.float32) * IHDIM ** (-0.5)
        scores = jnp.where(causal, scores, -jnp.inf)
        top = lax.optimization_barrier(jnp.max(scores, axis=1, keepdims=True))
        expo = jnp.exp(scores - top)
        probs = (expo / lax.optimization_barrier(jnp.sum(expo, axis=1, keepdims=True))).astype(jnp.bfloat16)
        heads_out = jnp.dot(probs, values, preferred_element_type=jnp.float32).astype(jnp.bfloat16)
        return (total + jnp.dot(heads_out, w_out, preferred_element_type=jnp.float32), None)
    back, _ = lax.scan(one_head, jnp.zeros((NCH, D), jnp.float32), (qkv_weight, attn_out))
    return hidden.astype(jnp.float32).at[group_pos].add(back).astype(jnp.bfloat16)
```

```python
import functools

import jax
import jax.numpy as jnp
from jax import lax
from jax.experimental import pallas as pl
from jax.experimental.pallas import tpu as pltpu
from jax.sharding import PartitionSpec as P

F32 = jnp.float32
BF16 = jnp.bfloat16
EPS = 1e-05
VMEM = pl.BlockSpec(memory_space=pltpu.VMEM)
ANY = pl.BlockSpec(memory_space=pl.ANY)


def dot(a, b):
    return jnp.dot(a, b, preferred_element_type=F32)


def dot_rows(a, b):
    return lax.dot_general(a, b, (((0,), (0,)), ((), ())), preferred_element_type=F32)


def dot_lanes(a, b):
    return lax.dot_general(a, b, (((1,), (1,)), ((), ())), preferred_element_type=F32)


def iota(shape, axis):
    return lax.broadcasted_iota(jnp.int32, shape, axis)


def terms(value, count):
    out = []
    for _ in range(count):
        term = value.astype(BF16)
        out.append(term)
        value = value - term.astype(F32)
    return out


def spread(value, heads, width, count):
    size = width // heads
    row = iota((heads, width), 0)
    lane = iota((heads, width), 1)
    pick = ((lane >= row * size) & (lane < (row + 1) * size)).astype(BF16)
    return sum(dot(term, pick) for term in terms(value, count))


def weight_copies(weight, buffer, sems, start, step):
    count = buffer.shape[0]
    return [
        pltpu.make_async_copy(
            weight.at[:, pl.ds(start + i * step, step)], buffer.at[i], sems.at[i]
        )
        for i in range(count)
    ]


def front_kernel(
    split, tokens, decay, weight, qkv, attn_out,
    xs, bc, local, first, total, cumul, piece,
    xs_buffer, bc_buffer, xs_sems, bc_sems,
):
    length, heads = decay.shape
    width = xs.shape[1]
    states = local.shape[0]
    step = xs_buffer.shape[2]
    bc_copy = weight_copies(weight, bc_buffer, bc_sems, 2 * width, 2 * states)
    xs_copy = weight_copies(weight, xs_buffer, xs_sems, 0, step)
    for copy in bc_copy + xs_copy:
        copy.start()

    lower = (iota((length, length), 0) >= iota((length, length), 1)).astype(BF16)
    cum = sum(dot(lower, term) for term in terms(decay[...], 3))
    cumul[...] = cum
    last = cum[length - 1 :, :]
    tails = jnp.exp(last - cum)
    total[...] = spread(jnp.broadcast_to(jnp.exp(last), (8, heads)), heads, width, 3)
    tails_wide = spread(tails, heads, width, 2)

    mine = lax.rem(lax.axis_index("grp"), split)
    rows = qkv.shape[1] // split
    part = qkv[0, pl.ds(pl.multiple_of(mine * rows, rows), rows), :]
    two = 2 * part.shape[1] // 3
    value = part[:, two:]
    half = rows // 2
    piece[:rows, :] = part[:, :two]
    piece[rows : rows + half, :] = jnp.concatenate([value[:half], value[half:]], axis=1)
    few = attn_out.shape[1] // split
    back = attn_out[0, pl.ds(pl.multiple_of(mine * few, few), few), :]
    for i in range(back.shape[1] // two):
        at = rows + half + i * few
        piece[at : at + few, :] = back[:, i * two : (i + 1) * two]

    bc_copy[0].wait()
    ins = tokens[...]
    both = dot(ins, bc_buffer[0]).astype(BF16)
    bc[...] = both
    for i, copy in enumerate(xs_copy):
        lanes = slice(i * step, (i + 1) * step)
        copy.wait()
        block = dot(ins, xs_buffer[i]).astype(BF16)
        xs[:, lanes] = block
        scaled = (block.astype(F32) * tails_wide[:, lanes]).astype(BF16)
        state = dot_rows(both, scaled)[:states]
        local[:, lanes] = state
        first[:, lanes] = state.astype(BF16)


def middle_kernel(
    tokens, decay, weight, cumul, xs, bc, groups,
    within, silu, grown, placing, cmat,
    gate_buffer, gate_sems,
):
    length, heads = decay.shape
    width = xs.shape[1]
    states = bc.shape[1] // 2
    step = gate_buffer.shape[2]
    most = placing.shape[1]
    copies = weight_copies(weight, gate_buffer, gate_sems, width, step)
    for copy in copies:
        copy.start()

    here = lax.axis_index("seq") * length
    count = groups.shape[1]
    position = here + iota((length, count), 0)
    group = jnp.broadcast_to(groups[...], (length, count))
    starts = jnp.sum((group == position).astype(F32), axis=1, keepdims=True)
    ahead = (group < position) & (group >= here)
    rank = jnp.sum(ahead.astype(F32), axis=1, keepdims=True).astype(jnp.int32)
    slot = iota((length, most), 1)
    placing[...] = jnp.where(slot == rank, starts, 0.0).astype(BF16)

    cum = cumul[...]
    upper = (iota((length, length), 0) <= iota((length, length), 1)).astype(BF16)
    cum_t = sum(dot_rows(term, upper) for term in terms(decay[...], 3))
    grown[...] = spread(jnp.exp(cum), heads, width, 2)
    both = bc[...]
    cmat[...] = both[:, states:]
    mixed = dot_lanes(both[:, states:], both[:, :states])

    half = length // 2
    lower = iota((half, half), 0) >= iota((half, half), 1)
    size = width // heads
    pair = 2 * size
    left = iota((half, pair), 1) < size
    for at in range(0, heads, 2):
        lanes = slice(at * size, at * size + pair)
        early, late = xs[:half, lanes], xs[half:, lanes]
        tops, lows = [], []
        for head in (at, at + 1):
            column = cum[:, head : head + 1]
            row = cum_t[head : head + 1, :]
            apart = jnp.where(lower, column[:half] - row[:, :half], -jnp.inf)
            top = (jnp.exp(apart) * mixed[:half, :half]).astype(BF16)
            apart = jnp.where(lower, column[half:] - row[:, half:], -jnp.inf)
            low = (jnp.exp(apart) * mixed[half:, half:]).astype(BF16)
            across = jnp.exp(column[half:] - row[:, :half])
            across = (across * mixed[half:, :half]).astype(BF16)
            tops.append(dot(top, early))
            lows.append(dot(low, late) + dot(across, early))
        within[:half, lanes] = jnp.where(left, tops[0], tops[1])
        within[half:, lanes] = jnp.where(left, lows[0], lows[1])

    ins = tokens[...]
    for i, copy in enumerate(copies):
        copy.wait()
        gate = dot(ins, gate_buffer[i]).astype(BF16).astype(F32)
        silu[:, i * step : (i + 1) * step] = gate / (1.0 + jnp.exp(-gate))


def post_kernel(
    state, within, silu, grown, placing, cmat, gain, out_weight, tokens, inner_gain,
    hidden, rows,
):
    carried = dot(cmat[...], state[...])
    gated = (within[...] + grown[...] * carried) * silu[...]
    scale = lax.rsqrt(jnp.mean(gated * gated, axis=1, keepdims=True) + EPS)
    normed = (gated * scale * gain[...]).astype(BF16)
    mixed = dot(normed, out_weight[...])
    out = (tokens[...].astype(F32) + mixed).astype(BF16)
    hidden[...] = out
    picked = dot_rows(placing[...], out)
    scale = lax.rsqrt(jnp.mean(picked * picked, axis=1, keepdims=True) + EPS)
    rows[...] = (picked * scale * inner_gain[...]).astype(BF16)


def weight_kernel(masks, split, model, head_dim, *refs):
    count = len(masks)
    bundles, (wq, wk, wv, wo) = refs[:count], refs[count:]
    heads = wq.shape[1] // head_dim
    rows = model // split
    half = rows // 2
    few = head_dim // split
    two = 2 * head_dim
    tall = rows + half + few * (model // two)
    mine = lax.rem(lax.axis_index("grp"), split)
    for bundle, mask in zip(bundles, masks):
        for j, bits in enumerate(mask):
            quarter = mine ^ bits
            down = pl.ds(pl.multiple_of(quarter * rows, rows), rows)
            for h in range(heads):
                at = (j * heads + h) * tall
                lanes = slice(h * head_dim, (h + 1) * head_dim)
                both = bundle[at : at + rows, :]
                wq[down, lanes] = both[:, :head_dim]
                wk[down, lanes] = both[:, head_dim:]
                value = bundle[at + rows : at + rows + half, :]
                wv[down, lanes] = jnp.concatenate([value[:, :head_dim], value[:, head_dim:]], axis=0)
                at += rows + half
                start = pl.multiple_of(h * head_dim + quarter * few, few)
                for i in range(model // two):
                    wo[pl.ds(start, few), i * two : (i + 1) * two] = bundle[
                        at + i * few : at + (i + 1) * few, :
                    ]


def attend_kernel(devices, length, *refs):
    rows = refs[:devices]
    wq, wk, wv, wo, hidden, placing, groups, result = refs[devices:]
    most = rows[0].shape[0]
    heads = devices
    head_dim = wq.shape[1] // heads
    me = lax.axis_index("seq")
    own = rows[0][...]
    known = jnp.concatenate([own] + [row[...] for row in rows[1:]], axis=0)
    query = dot(own, wq[...]).astype(BF16)
    keys = dot(known, wk[...]).astype(BF16)
    values = dot(known, wv[...]).astype(BF16)

    slot = iota((most, most), 1)
    allowed = [slot <= iota((most, most), 0)]
    for back in range(1, devices):
        start = (me - back) * length
        inside = (groups[...] >= start) & (groups[...] < start + length)
        count = jnp.sum(inside.astype(F32), axis=1, keepdims=True).astype(jnp.int32)
        allowed.append(slot < count)
    allowed = jnp.concatenate(allowed, axis=1)

    outs = []
    for head in range(heads):
        lanes = slice(head * head_dim, (head + 1) * head_dim)
        scores = dot_lanes(query[:, lanes], keys[:, lanes]) * head_dim ** (-0.5)
        scores = jnp.where(allowed, scores, -jnp.inf)
        top = jnp.max(scores, axis=1, keepdims=True)
        expo = jnp.exp(scores - top)
        probs = (expo / jnp.sum(expo, axis=1, keepdims=True)).astype(BF16)
        outs.append(dot(probs, values[:, lanes]).astype(BF16))
    joined = jnp.concatenate(outs, axis=1)
    back = dot(joined, wo[...])
    place = placing[...]
    placed = sum(dot(place, term) for term in terms(back, 2))
    result[...] = (hidden[...].astype(F32) + placed).astype(BF16)


def call(kernel, outs, ins, scratch=(), specs=None):
    return pl.pallas_call(
        kernel,
        out_shape=[jax.ShapeDtypeStruct(shape, dtype) for shape, dtype in outs],
        in_specs=specs or [VMEM] * len(ins),
        out_specs=[VMEM] * len(outs),
        scratch_shapes=list(scratch),
    )(*ins)


def shards(
    tokens, group_pos, log_decay, in_weight, norm_gain, out_weight, inner_gain, qkv_weight, attn_out
):
    devices = lax.axis_size("seq")
    grps = lax.axis_size("grp")
    length, model = tokens.shape
    heads = log_decay.shape[1]
    width = out_weight.shape[0]
    states = (in_weight.shape[1] - 2 * width) // 2
    head_dim = attn_out.shape[1]
    most = length // 2
    split = next(s for s in (4, 2, 1) if grps % s == 0)
    step = min(256, width)
    chunks = width // step
    groups = group_pos.reshape(1, -1)
    tall = model // split * 3 // 2 + head_dim // split * (model // (2 * head_dim))

    xs, bc, local, first, total, cumul, piece = call(
        functools.partial(front_kernel, split),
        [
            ((length, width), BF16),
            ((length, 2 * states), BF16),
            ((states, width), F32),
            ((states, width), BF16),
            ((8, width), F32),
            ((length, heads), F32),
            ((tall, 2 * head_dim), BF16),
        ],
        [tokens, log_decay, in_weight, qkv_weight, attn_out],
        [
            pltpu.VMEM((chunks, model, step), BF16),
            pltpu.VMEM((1, model, 2 * states), BF16),
            pltpu.SemaphoreType.DMA((chunks,)),
            pltpu.SemaphoreType.DMA((1,)),
        ],
        [VMEM, VMEM, ANY, VMEM, VMEM],
    )

    state = jnp.zeros((states, width), BF16)
    for s in range(devices - 1):
        sent = first
        if s:
            sent = (total[:1] * state.astype(F32) + local).astype(BF16)
        state = state + lax.ppermute(sent, "seq", [(s, s + 1)])

    within, silu, grown, placing, cmat = call(
        middle_kernel,
        [
            ((length, width), F32),
            ((length, width), F32),
            ((length, width), F32),
            ((length, most), BF16),
            ((length, states), BF16),
        ],
        [tokens, log_decay, in_weight, cumul, xs, bc, groups],
        [pltpu.VMEM((chunks, model, step), BF16), pltpu.SemaphoreType.DMA((chunks,))],
        [VMEM, VMEM, ANY, VMEM, VMEM, VMEM, VMEM],
    )

    pieces = [piece]
    for s in range(1, devices):
        around = [(i, (i + s) % devices) for i in range(devices)]
        pieces.append(lax.ppermute(piece, "seq", around))
    bundles, masks, bit = [jnp.concatenate(pieces, axis=0)], [(0,)], split // 2
    while bit:
        whole = bundles[0] if len(bundles) == 1 else jnp.concatenate(bundles, axis=0)
        other = lax.ppermute(whole, "grp", [(i, i ^ bit) for i in range(grps)])
        bundles.append(other)
        masks.append(tuple(m ^ bit for mask in masks for m in mask))
        bit //= 2
    weights = call(
        functools.partial(weight_kernel, masks, split, model, head_dim),
        [((model, devices * head_dim), BF16)] * 3 + [((devices * head_dim, model), BF16)],
        bundles,
    )

    hidden, rows = call(
        post_kernel,
        [((length, model), BF16), ((most, model), BF16)],
        [
            state, within, silu, grown, placing, cmat, norm_gain.reshape(1, -1), out_weight,
            tokens, inner_gain.reshape(1, -1),
        ],
    )
    known = [rows]
    for s in range(1, devices):
        known.append(lax.ppermute(rows, "seq", [(i, i + s) for i in range(devices - s)]))

    (result,) = call(
        functools.partial(attend_kernel, devices, length),
        [((length, model), BF16)],
        known + list(weights) + [hidden, placing, groups],
    )
    return result


def solution(mesh):
    in_specs = (
        P(("grp", "seq"), None),
        P("grp"),
        P(("grp", "seq"), None),
        P(),
        P(),
        P(),
        P(),
        P("seq", None, None),
        P("seq", None, None),
    )
    out_specs = P(("grp", "seq"), None)
    return jax.shard_map(shards, mesh=mesh, in_specs=in_specs, out_specs=out_specs, check_vma=False)
```

```python
import functools

import jax
import jax.numpy as jnp
from jax import lax
from jax.experimental import pallas as pl
from jax.experimental.pallas import tpu as pltpu
from jax.sharding import PartitionSpec as P


F32 = jnp.float32
BF16 = jnp.bfloat16
EPS = 1e-05
VMEM = pl.BlockSpec(memory_space=pltpu.VMEM)
HBM = pl.BlockSpec(memory_space=pltpu.HBM)


def dot(a, b):
    return jnp.dot(a, b, preferred_element_type=F32)


def dot_rows(a, b):
    return lax.dot_general(a, b, (((0,), (0,)), ((), ())), preferred_element_type=F32)


def dot_lanes(a, b):
    return lax.dot_general(a, b, (((1,), (1,)), ((), ())), preferred_element_type=F32)


def iota(shape, axis):
    return lax.broadcasted_iota(jnp.int32, shape, axis)


def terms(value, count):
    out = []
    for _ in range(count):
        term = value.astype(BF16)
        out.append(term)
        value = value - term.astype(F32)
    return out


def spread(value, heads, width, count):
    size = width // heads
    row = iota((heads, width), 0)
    lane = iota((heads, width), 1)
    pick = ((lane >= row * size) & (lane < (row + 1) * size)).astype(BF16)
    return sum(dot(term, pick) for term in terms(value, count))


def weight_copies(weight, buffer, sems, start, step):
    count = buffer.shape[0]
    return [
        pltpu.make_async_copy(
            weight.at[:, pl.ds(start + i * step, step)], buffer.at[i], sems.at[i]
        )
        for i in range(count)
    ]


def front_kernel(
    tokens_hbm, decay_hbm, weight,
    xs, bc, local, first, total, cumul,
    tokens, decay, xs_buffer, bc_buffer, small_sems, xs_sems, bc_sems,
):
    heads, length = decay.shape
    width = xs.shape[1]
    states = local.shape[0]
    step = xs_buffer.shape[2]
    bc_copy = weight_copies(weight, bc_buffer, bc_sems, 2 * width, 2 * states)
    xs_copy = weight_copies(weight, xs_buffer, xs_sems, 0, step)
    decay_copy = pltpu.make_async_copy(decay_hbm, decay, small_sems.at[0])
    token_copy = pltpu.make_async_copy(tokens_hbm, tokens, small_sems.at[1])
    for copy in [decay_copy, token_copy] + bc_copy + xs_copy:
        copy.start()

    decay_copy.wait()
    lower = (iota((length, length), 0) >= iota((length, length), 1)).astype(BF16)
    cum = sum(dot_lanes(lower, term) for term in terms(decay[...], 3))
    cumul[...] = cum
    last = cum[length - 1 :, :]
    tails = jnp.exp(last - cum)
    total[...] = spread(jnp.broadcast_to(jnp.exp(last), (8, heads)), heads, width, 3)
    tails_wide = spread(tails, heads, width, 2)

    token_copy.wait()
    bc_copy[0].wait()
    ins = tokens[...]
    both = dot(ins, bc_buffer[0]).astype(BF16)
    bc[...] = both
    for i, copy in enumerate(xs_copy):
        lanes = slice(i * step, (i + 1) * step)
        copy.wait()
        block = dot(ins, xs_buffer[i]).astype(BF16)
        xs[:, lanes] = block
        scaled = (block.astype(F32) * tails_wide[:, lanes]).astype(BF16)
        state = dot_rows(both, scaled)[:states]
        local[:, lanes] = state
        first[:, lanes] = state.astype(BF16)


def middle_kernel(
    split, tokens, decay, weight, cumul, xs, bc, groups, qkv, attn_out,
    within, silu, grown, placing, cmat, piece,
    gate_buffer, gate_sems,
):
    heads, length = decay.shape
    width = xs.shape[1]
    states = bc.shape[1] // 2
    step = gate_buffer.shape[2]
    most = placing.shape[1]
    copies = weight_copies(weight, gate_buffer, gate_sems, width, step)
    for copy in copies:
        copy.start()

    mine = lax.rem(lax.axis_index("grp"), split[0] * split[1])
    lanes = piece.shape[1]
    column = pl.ds(pl.multiple_of(lax.rem(mine, split[0]) * lanes, lanes), lanes)
    stack = jnp.concatenate([qkv[0, :, column], attn_out[0, :, column]], axis=0)
    tall = piece.shape[0]
    part = lax.div(mine, split[0])
    chosen = stack[:tall]
    for i in range(1, split[1]):
        chosen = jnp.where(part == i, stack[i * tall : (i + 1) * tall], chosen)
    piece[...] = chosen

    here = lax.axis_index("seq") * length
    count = groups.shape[1]
    position = here + iota((length, count), 0)
    group = jnp.broadcast_to(groups[...], (length, count))
    starts = jnp.sum((group == position).astype(F32), axis=1, keepdims=True)
    ahead = (group < position) & (group >= here)
    rank = jnp.sum(ahead.astype(F32), axis=1, keepdims=True).astype(jnp.int32)
    slot = iota((length, most), 1)
    placing[...] = jnp.where(slot == rank, starts, 0.0).astype(BF16)

    cum = cumul[...]
    upper = (iota((length, length), 0) <= iota((length, length), 1)).astype(BF16)
    cum_t = sum(dot(term, upper) for term in terms(decay[...], 3))
    grown[...] = spread(jnp.exp(cum), heads, width, 2)
    both = bc[...]
    cmat[...] = both[:, states:]
    mixed = dot_lanes(both[:, states:], both[:, :states])

    half = length // 2
    lower = iota((half, half), 0) >= iota((half, half), 1)
    size = width // heads
    pair = 2 * size
    left = iota((half, pair), 1) < size
    for at in range(0, heads, 2):
        lanes = slice(at * size, at * size + pair)
        early, late = xs[:half, lanes], xs[half:, lanes]
        tops, lows = [], []
        for head in (at, at + 1):
            column = cum[:, head : head + 1]
            row = cum_t[head : head + 1, :]
            apart = jnp.where(lower, column[:half] - row[:, :half], -jnp.inf)
            top = (jnp.exp(apart) * mixed[:half, :half]).astype(BF16)
            apart = jnp.where(lower, column[half:] - row[:, half:], -jnp.inf)
            low = (jnp.exp(apart) * mixed[half:, half:]).astype(BF16)
            across = jnp.exp(column[half:] - row[:, :half])
            across = (across * mixed[half:, :half]).astype(BF16)
            tops.append(dot(top, early))
            lows.append(dot(low, late) + dot(across, early))
        within[:half, lanes] = jnp.where(left, tops[0], tops[1])
        within[half:, lanes] = jnp.where(left, lows[0], lows[1])

    ins = tokens[...]
    for i, copy in enumerate(copies):
        copy.wait()
        gate = dot(ins, gate_buffer[i]).astype(BF16).astype(F32)
        silu[:, i * step : (i + 1) * step] = gate / (1.0 + jnp.exp(-gate))


def merge_kernel(step, came, before, total, local, state, sent):
    taken = lax.axis_index("seq") == step + 1
    value = jnp.where(taken, came[...].astype(F32), before[...].astype(F32))
    state[...] = value.astype(BF16)
    sent[...] = (total[0:1, :] * value + local[...]).astype(BF16)


def first_merge_kernel(step, came, total, local, state, sent):
    taken = lax.axis_index("seq") == step + 1
    value = jnp.where(taken, came[...].astype(F32), 0.0)
    state[...] = value.astype(BF16)
    sent[...] = (total[0:1, :] * value + local[...]).astype(BF16)


def post_kernel(
    low, high, state, within, silu, grown, placing, cmat, gain, out_weight, tokens, inner_gain,
    *refs,
):
    earlier, (hidden, rows) = refs[:-2], refs[-2:]
    me = lax.axis_index("seq")
    active = (me >= low) & (me < high)

    @pl.when(active)
    def _():
        carried = dot(cmat[...], state[...])
        gated = (within[...] + grown[...] * carried) * silu[...]
        scale = lax.rsqrt(jnp.mean(gated * gated, axis=1, keepdims=True) + EPS)
        normed = (gated * scale * gain[...]).astype(BF16)
        mixed = dot(normed, out_weight[...])
        out = (tokens[...].astype(F32) + mixed).astype(BF16)
        hidden[...] = out
        picked = dot_rows(placing[...], out)
        scale = lax.rsqrt(jnp.mean(picked * picked, axis=1, keepdims=True) + EPS)
        rows[...] = (picked * scale * inner_gain[...]).astype(BF16)

    @pl.when(jnp.logical_not(active))
    def _():
        hidden[...] = earlier[0][...] if earlier else jnp.zeros_like(hidden)
        rows[...] = earlier[1][...] if earlier else jnp.zeros_like(rows)


def weight_kernel(masks, split, *refs):
    bundles, out = refs[:-1], refs[-1]
    parts = out.shape[0] // split[1]
    lanes = bundles[0].shape[1]
    mine = lax.rem(lax.axis_index("grp"), split[0] * split[1])
    tall = out.shape[1]
    for bundle, mask in zip(bundles, masks):
        source = mine ^ mask
        column = pl.ds(pl.multiple_of(lax.rem(source, split[0]) * lanes, lanes), lanes)
        part = lax.div(source, split[0]) * parts
        for j in range(parts):
            out[part + j, :, column] = bundle[j * tall : (j + 1) * tall, :]


def attend_kernel(devices, length, *refs):
    known, (hidden, weights, placing, groups, result) = refs[:devices], refs[devices:]
    most = known[0].shape[0]
    heads = devices
    head_dim = weights.shape[1] // heads
    me = lax.axis_index("seq")
    own = known[0][...]
    known = jnp.concatenate([block[...] for block in known], axis=0)
    query = dot_lanes(own, weights[0]).astype(BF16)
    keys = dot_lanes(weights[1], known).astype(BF16)
    values = dot_lanes(known, weights[2]).astype(BF16)

    slot = iota((most, most), 1)
    allowed = [slot <= iota((most, most), 0)]
    for back in range(1, devices):
        other = me ^ back
        start = other * length
        inside = (groups[...] >= start) & (groups[...] < start + length)
        count = jnp.sum(inside.astype(F32), axis=1, keepdims=True).astype(jnp.int32)
        allowed.append(slot < jnp.where(other < me, count, 0))
    allowed = jnp.concatenate(allowed, axis=1)

    outs = []
    for head in range(heads):
        lanes = slice(head * head_dim, (head + 1) * head_dim)
        scores = dot(query[:, lanes], keys[lanes, :]) * head_dim ** (-0.5)
        scores = jnp.where(allowed, scores, -jnp.inf)
        top = jnp.max(scores, axis=1, keepdims=True)
        expo = jnp.exp(scores - top)
        probs = (expo / jnp.sum(expo, axis=1, keepdims=True)).astype(BF16)
        outs.append(dot(probs, values[:, lanes]).astype(BF16))
    joined = jnp.concatenate(outs, axis=1)
    back = dot(joined, weights[3])
    place = placing[...]
    placed = sum(dot(place, term) for term in terms(back, 2))
    result[...] = (hidden[...].astype(F32) + placed).astype(BF16)


def swap(value, axis, mask):
    pairs = [(i, i ^ mask) for i in range(lax.axis_size(axis))]
    return lax.ppermute(value, axis, pairs)


def in_hbm(value):
    return pltpu.with_memory_space_constraint(value, pltpu.HBM)


def call(kernel, outs, ins, cost, scratch=(), specs=None):
    kernel = pl.pallas_call(
        kernel,
        out_shape=[jax.ShapeDtypeStruct(shape, dtype) for shape, dtype in outs],
        in_specs=specs or [VMEM] * len(ins),
        out_specs=[VMEM] * len(outs),
        scratch_shapes=list(scratch),
        cost_estimate=pl.CostEstimate(flops=cost, transcendentals=0, bytes_accessed=0),
        compiler_params=pltpu.CompilerParams(vmem_limit_bytes=24 << 20),
    )
    return kernel(*ins)


def shards(
    tokens, group_pos, log_decay, in_weight, norm_gain, out_weight, inner_gain, qkv_weight, attn_out
):
    devices = lax.axis_size("seq")
    grps = lax.axis_size("grp")
    length, model = tokens.shape
    heads = log_decay.shape[1]
    width = out_weight.shape[0]
    states = (in_weight.shape[1] - 2 * width) // 2
    head_dim = attn_out.shape[1]
    most = length // 2
    lane_split = next(s for s in (4, 2, 1) if grps % s == 0 and model % (128 * s) == 0)
    row_split = 2 if grps % (2 * lane_split) == 0 else 1
    split = (lane_split, row_split)
    tall = 4 * head_dim // row_split
    step = min(256, width)
    chunks = width // step
    groups = group_pos.reshape(1, -1)
    decay = log_decay.T
    qkv = jnp.transpose(qkv_weight, (0, 2, 1))
    gain, inner = norm_gain.reshape(1, -1), inner_gain.reshape(1, -1)
    buffers = [pltpu.VMEM((chunks, model, step), BF16), pltpu.SemaphoreType.DMA((chunks,))]

    xs, bc, local, first, total, cumul = call(
        front_kernel,
        [
            ((length, width), BF16),
            ((length, 2 * states), BF16),
            ((states, width), F32),
            ((states, width), BF16),
            ((8, width), F32),
            ((length, heads), F32),
        ],
        [in_hbm(tokens), in_hbm(decay), in_hbm(in_weight)],
        3 * 10**9,
        [
            pltpu.VMEM(tokens.shape, BF16),
            pltpu.VMEM(decay.shape, F32),
            buffers[0],
            pltpu.VMEM((1, model, 2 * states), BF16),
            pltpu.SemaphoreType.DMA((2,)),
            buffers[1],
            pltpu.SemaphoreType.DMA((1,)),
        ],
        [HBM, HBM, HBM],
    )

    def link(sent, step):
        pairs = [(step, step + 1), (step + 1, step)]
        return lax.ppermute(sent, "seq", pairs)

    came = link(first, 0)

    within, silu, grown, placing, cmat, piece = call(
        functools.partial(middle_kernel, split),
        [
            ((length, width), F32),
            ((length, width), F32),
            ((length, width), F32),
            ((length, most), BF16),
            ((length, states), BF16),
            ((tall, model // lane_split), BF16),
        ],
        [tokens, decay, in_hbm(in_weight), cumul, xs, bc, groups, qkv, attn_out],
        3 * 10**9,
        buffers,
        [VMEM, VMEM, HBM] + [VMEM] * 6,
    )

    pieces = [piece]
    for mask in range(1, devices):
        pieces.append(swap(piece, "seq", mask))
    bundle = jnp.concatenate(
        [p[i * head_dim : (i + 1) * head_dim] for i in range(tall // head_dim) for p in pieces], axis=0
    )
    bundles, masks = [bundle], [0]
    for mask in range(2, lane_split * row_split, 2):
        bundles.append(swap(bundle, "grp", mask))
        masks.append(mask)
    if lane_split > 1:
        for i in range(len(bundles)):
            bundles.append(swap(bundles[i], "grp", 1))
            masks.append(masks[i] ^ 1)
    (weights,) = call(
        functools.partial(weight_kernel, masks, split),
        [((4, devices * head_dim, model), BF16)],
        bundles,
        10**9,
    )

    state, kept, blocks, done = None, [], {}, 0
    bounds = stages(devices)
    for low, high in zip(bounds[:-1], bounds[1:]):
        while done < high - 1 and done < devices - 2:
            ins = [came] + ([] if state is None else [state]) + [total, local]
            kernel = functools.partial(first_merge_kernel if state is None else merge_kernel, done)
            state, sent = call(kernel, [((states, width), BF16)] * 2, ins, 10**8)
            done += 1
            came = link(sent, done)
        kept = call(
            functools.partial(post_kernel, low, high),
            [((length, model), BF16), ((most, model), BF16)],
            [came if high == devices else state, within, silu, grown, placing, cmat, gain]
            + [out_weight, tokens, inner]
            + list(kept),
            2 * 10**9,
        )
        if high < devices:
            for mask in range(devices // 2 if low == 0 else 1, devices):
                if mask not in blocks:
                    blocks[mask] = swap(kept[1], "seq", mask)

    known = [kept[1]] + [blocks[mask] for mask in range(1, devices)]
    (result,) = call(
        functools.partial(attend_kernel, devices, length),
        [((length, model), BF16)],
        known + [kept[0], weights, placing, groups],
        3 * 10**9,
    )
    return result


def stages(devices):
    return sorted({0, devices // 2, devices - 1, devices})


def solution(mesh):
    in_specs = (
        P(("grp", "seq"), None),
        P("grp"),
        P(("grp", "seq"), None),
        P(),
        P(),
        P(),
        P(),
        P("seq", None, None),
        P("seq", None, None),
    )
    out_specs = P(("grp", "seq"), None)
    return jax.shard_map(shards, mesh=mesh, in_specs=in_specs, out_specs=out_specs, check_vma=False)
```

```python
import functools

import jax
import jax.numpy as jnp
from jax import lax
from jax.experimental import pallas as pl
from jax.experimental.pallas import tpu as pltpu
from jax.sharding import PartitionSpec as P


F32 = jnp.float32
BF16 = jnp.bfloat16
EPS = 1e-05
VMEM = pl.BlockSpec(memory_space=pltpu.VMEM)
HBM = pl.BlockSpec(memory_space=pltpu.HBM)


def dot(a, b):
    return jnp.dot(a, b, preferred_element_type=F32)


def dot_rows(a, b):
    return lax.dot_general(a, b, (((0,), (0,)), ((), ())), preferred_element_type=F32)


def dot_lanes(a, b):
    return lax.dot_general(a, b, (((1,), (1,)), ((), ())), preferred_element_type=F32)


def iota(shape, axis):
    return lax.broadcasted_iota(jnp.int32, shape, axis)


def terms(value, count):
    out = []
    for _ in range(count):
        term = value.astype(BF16)
        out.append(term)
        value = value - term.astype(F32)
    return out


def spread(value, heads, width, count):
    size = width // heads
    row = lax.rem(iota((count * heads, width), 0), heads)
    lane = iota((count * heads, width), 1)
    pick = ((lane >= row * size) & (lane < (row + 1) * size)).astype(BF16)
    return dot(jnp.concatenate(terms(value, count), axis=1), pick)


def weight_copies(weight, buffer, sems, start, step):
    count = buffer.shape[0]
    return [
        pltpu.make_async_copy(
            weight.at[:, pl.ds(start + i * step, step)], buffer.at[i], sems.at[i]
        )
        for i in range(count)
    ]


def front_kernel(
    split, tokens_hbm, decay_hbm, weight, qkv, attn_out,
    xs, bc, local, first, total, cumul,
    tokens, decay, stack, xs_buffer, bc_buffer, small_sems, xs_sems, bc_sems,
):
    heads, length = decay.shape
    width = xs.shape[1]
    states = local.shape[0]
    step = xs_buffer.shape[2]
    bc_copy = weight_copies(weight, bc_buffer, bc_sems, 2 * width, 2 * states)
    xs_copy = weight_copies(weight, xs_buffer, xs_sems, 0, step)
    decay_copy = pltpu.make_async_copy(decay_hbm, decay, small_sems.at[0])
    token_copy = pltpu.make_async_copy(tokens_hbm, tokens, small_sems.at[1])
    mine = lax.rem(lax.axis_index("grp"), split[0] * split[1])
    lanes = stack.shape[1]
    column = pl.ds(pl.multiple_of(lax.rem(mine, split[0]) * lanes, lanes), lanes)
    upper_rows = qkv.shape[1]
    qkv_copy = pltpu.make_async_copy(
        qkv.at[0, :, column], stack.at[pl.ds(0, upper_rows)], small_sems.at[2]
    )
    out_copy = pltpu.make_async_copy(
        attn_out.at[0, :, column],
        stack.at[pl.ds(upper_rows, attn_out.shape[1])],
        small_sems.at[3],
    )
    for copy in [decay_copy, token_copy] + bc_copy + xs_copy + [qkv_copy, out_copy]:
        copy.start()

    decay_copy.wait()
    lower = (iota((length, length), 0) >= iota((length, length), 1)).astype(BF16)
    cum = sum(dot_lanes(lower, term) for term in terms(decay[...], 3))
    cumul[...] = cum
    last = cum[length - 1 :, :]
    tails = jnp.exp(last - cum)
    total[...] = spread(jnp.broadcast_to(jnp.exp(last), (8, heads)), heads, width, 3)
    tails_wide = spread(tails, heads, width, 2)

    token_copy.wait()
    bc_copy[0].wait()
    ins = tokens[...]
    both = dot(ins, bc_buffer[0]).astype(BF16)
    bc[...] = both
    for i, copy in enumerate(xs_copy):
        at = slice(i * step, (i + 1) * step)
        copy.wait()
        block = dot(ins, xs_buffer[i]).astype(BF16)
        xs[:, at] = block
        scaled = (block.astype(F32) * tails_wide[:, at]).astype(BF16)
        state = dot_rows(both, scaled)[:states]
        local[:, at] = state
        first[:states, at] = state.astype(BF16)

    qkv_copy.wait()
    out_copy.wait()
    tall = stack.shape[0] // split[1]
    part = lax.div(mine, split[0])
    piece = stack[pl.ds(pl.multiple_of(part * tall, tall), tall), :]
    few = first.shape[0] - states
    wide = stack.shape[1]
    for i in range(width // wide):
        first[states:, i * wide : (i + 1) * wide] = piece[i * few : (i + 1) * few]


def middle_kernel(
    tokens, decay, weight, cumul, xs, bc, groups,
    within, silu, grown, placing, cmat,
    gate_buffer, gate_sems,
):
    heads, length = decay.shape
    width = xs.shape[1]
    states = bc.shape[1] // 2
    step = gate_buffer.shape[2]
    most = placing.shape[1]
    copies = weight_copies(weight, gate_buffer, gate_sems, width, step)
    for copy in copies:
        copy.start()

    here = lax.axis_index("seq") * length
    count = groups.shape[1]
    position = here + iota((length, count), 0)
    group = jnp.broadcast_to(groups[...], (length, count))
    starts = jnp.sum((group == position).astype(F32), axis=1, keepdims=True)
    ahead = (group < position) & (group >= here)
    rank = jnp.sum(ahead.astype(F32), axis=1, keepdims=True).astype(jnp.int32)
    slot = iota((length, most), 1)
    placing[...] = jnp.where(slot == rank, starts, 0.0).astype(BF16)

    cum = cumul[...]
    upper = (iota((length, length), 0) <= iota((length, length), 1)).astype(BF16)
    cum_t = sum(dot(term, upper) for term in terms(decay[...], 3))
    grown[...] = spread(jnp.exp(cum), heads, width, 2)
    both = bc[...]
    cmat[...] = both[:, states:]
    mixed = dot_lanes(both[:, states:], both[:, :states])

    half = length // 2
    lower = iota((half, half), 0) >= iota((half, half), 1)
    size = width // heads
    pair = 2 * size
    left = iota((half, pair), 1) < size
    for at in range(0, heads, 2):
        lanes = slice(at * size, at * size + pair)
        early, late = xs[:half, lanes], xs[half:, lanes]
        tops, lows = [], []
        for head in (at, at + 1):
            column = cum[:, head : head + 1]
            row = cum_t[head : head + 1, :]
            apart = jnp.where(lower, column[:half] - row[:, :half], -jnp.inf)
            top = (jnp.exp(apart) * mixed[:half, :half]).astype(BF16)
            apart = jnp.where(lower, column[half:] - row[:, half:], -jnp.inf)
            low = (jnp.exp(apart) * mixed[half:, half:]).astype(BF16)
            across = jnp.exp(column[half:] - row[:, :half])
            across = (across * mixed[half:, :half]).astype(BF16)
            tops.append(dot(top, early))
            lows.append(dot(low, late) + dot(across, early))
        within[:half, lanes] = jnp.where(left, tops[0], tops[1])
        within[half:, lanes] = jnp.where(left, lows[0], lows[1])

    ins = tokens[...]
    for i, copy in enumerate(copies):
        copy.wait()
        gate = dot(ins, gate_buffer[i]).astype(BF16).astype(F32)
        silu[:, i * step : (i + 1) * step] = gate / (1.0 + jnp.exp(-gate))


def merge_kernel(step, came, before, total, local, state, sent):
    taken = lax.axis_index("seq") == step + 1
    value = jnp.where(taken, came[...].astype(F32), before[...].astype(F32))
    state[...] = value.astype(BF16)
    sent[...] = (total[0:1, :] * value + local[...]).astype(BF16)


def first_merge_kernel(step, came, first, total, local, state, sent, bundle):
    taken = lax.axis_index("seq") == step + 1
    states = local.shape[0]
    value = jnp.where(taken, came[:states, :].astype(F32), 0.0)
    state[...] = value.astype(BF16)
    sent[...] = (total[0:1, :] * value + local[...]).astype(BF16)
    few = came.shape[0] - states
    wide = bundle.shape[1]
    count = local.shape[1] // wide
    for j, source in enumerate((first, came)):
        for i in range(count):
            at = (j * count + i) * few
            bundle[at : at + few, :] = source[states:, i * wide : (i + 1) * wide]


def post_kernel(
    low, high, state, within, silu, grown, placing, cmat, gain, out_weight, tokens, inner_gain,
    *refs,
):
    earlier, (hidden, rows) = refs[:-2], refs[-2:]
    me = lax.axis_index("seq")
    active = (me >= low) & (me < high)

    @pl.when(active)
    def _():
        carried = dot(cmat[...], state[...])
        gated = (within[...] + grown[...] * carried) * silu[...]
        scale = lax.rsqrt(jnp.mean(gated * gated, axis=1, keepdims=True) + EPS)
        normed = (gated * scale * gain[...]).astype(BF16)
        mixed = dot(normed, out_weight[...])
        out = (tokens[...].astype(F32) + mixed).astype(BF16)
        hidden[...] = out
        picked = dot_rows(placing[...], out)
        scale = lax.rsqrt(jnp.mean(picked * picked, axis=1, keepdims=True) + EPS)
        rows[...] = (picked * scale * inner_gain[...]).astype(BF16)

    @pl.when(jnp.logical_not(active))
    def _():
        hidden[...] = earlier[0][...] if earlier else jnp.zeros_like(hidden)
        rows[...] = earlier[1][...] if earlier else jnp.zeros_like(rows)


def weight_kernel(masks, split, head_dim, *refs):
    bundles, out = refs[:-1], refs[-1]
    parts = out.shape[0] // split[1]
    lanes = bundles[0].shape[1]
    mine = lax.rem(lax.axis_index("grp"), split[0] * split[1])
    heads = out.shape[1] // head_dim
    for bundle, mask in zip(bundles, masks):
        source = mine ^ mask
        column = pl.ds(pl.multiple_of(lax.rem(source, split[0]) * lanes, lanes), lanes)
        part = lax.div(source, split[0]) * parts
        for head in range(heads):
            for j in range(parts):
                at = (head * parts + j) * head_dim
                out[part + j, head * head_dim : (head + 1) * head_dim, column] = bundle[
                    at : at + head_dim, :
                ]


def own_kernel(devices, length, rows, weights, groups, query, keys, values, bias):
    most = rows.shape[0]
    own = rows[...]
    query[...] = dot_lanes(own, weights[0]).astype(BF16)
    keys[...] = dot_lanes(weights[1], own).astype(BF16)
    values[...] = dot_lanes(own, weights[2]).astype(BF16)
    me = lax.axis_index("seq")
    slot = iota((most, most), 1)
    bias[:, :most] = jnp.where(slot <= iota((most, most), 0), 0.0, -jnp.inf)
    for back in range(1, devices):
        other = me ^ back
        start = other * length
        inside = (groups[...] >= start) & (groups[...] < start + length)
        count = jnp.sum(inside.astype(F32), axis=1, keepdims=True).astype(jnp.int32)
        seen = slot < jnp.where(other < me, count, 0)
        bias[:, back * most : (back + 1) * most] = jnp.where(seen, 0.0, -jnp.inf)


def project_kernel(*refs):
    rows, (weights, keys, values) = refs[:-3], refs[-3:]
    block = sum(some[...] for some in rows)
    keys[...] = dot_lanes(weights[1], block).astype(BF16)
    values[...] = dot_lanes(block, weights[2]).astype(BF16)


def attend_kernel(devices, *refs):
    keys, refs = refs[:devices], refs[devices:]
    values, refs = refs[:devices], refs[devices:]
    query, bias, weights, hidden, placing, result = refs
    heads = devices
    head_dim = query.shape[1] // heads
    known = jnp.concatenate([block[...] for block in keys], axis=1)
    worth = jnp.concatenate([block[...] for block in values], axis=0)
    hide = bias[...]
    outs = []
    for head in range(heads):
        lanes = slice(head * head_dim, (head + 1) * head_dim)
        scores = dot(query[:, lanes], known[lanes, :]) * head_dim ** (-0.5) + hide
        top = jnp.max(scores, axis=1, keepdims=True)
        expo = jnp.exp(scores - top)
        share = 1.0 / jnp.sum(expo, axis=1, keepdims=True)
        outs.append(dot((expo * share).astype(BF16), worth[:, lanes]).astype(BF16))
    joined = jnp.concatenate(outs, axis=1)
    back = jnp.concatenate(terms(dot(joined, weights[3]), 2), axis=0)
    place = placing[...]
    placed = dot(jnp.concatenate([place, place], axis=1), back)
    result[...] = (hidden[...].astype(F32) + placed).astype(BF16)


def swap(value, axis, mask):
    pairs = [(i, i ^ mask) for i in range(lax.axis_size(axis))]
    return lax.ppermute(value, axis, pairs)


def in_hbm(value):
    return pltpu.with_memory_space_constraint(value, pltpu.HBM)


def call(kernel, outs, ins, cost, scratch=(), specs=None):
    kernel = pl.pallas_call(
        kernel,
        out_shape=[jax.ShapeDtypeStruct(shape, dtype) for shape, dtype in outs],
        in_specs=specs or [VMEM] * len(ins),
        out_specs=[VMEM] * len(outs),
        scratch_shapes=list(scratch),
        cost_estimate=pl.CostEstimate(flops=cost, transcendentals=0, bytes_accessed=0),
        compiler_params=pltpu.CompilerParams(vmem_limit_bytes=24 << 20),
    )
    return kernel(*ins)


def shards(
    tokens, group_pos, log_decay, in_weight, norm_gain, out_weight, inner_gain, qkv_weight, attn_out
):
    devices = lax.axis_size("seq")
    grps = lax.axis_size("grp")
    length, model = tokens.shape
    heads = log_decay.shape[1]
    width = out_weight.shape[0]
    states = (in_weight.shape[1] - 2 * width) // 2
    head_dim = attn_out.shape[1]
    most = length // 2
    lane_split = next(s for s in (4, 2, 1) if grps % s == 0 and model % (128 * s) == 0)
    row_split = 2 if grps % (2 * lane_split) == 0 else 1
    split = (lane_split, row_split)
    tall = 4 * head_dim // row_split
    lane_count = model // lane_split
    extra = tall * lane_count // width
    step = min(256, width)
    chunks = width // step
    wide = min(512, width)
    groups = group_pos.reshape(1, -1)
    decay = log_decay.T
    qkv = jnp.transpose(qkv_weight, (0, 2, 1))
    gain, inner = norm_gain.reshape(1, -1), inner_gain.reshape(1, -1)
    buffers = [pltpu.VMEM((chunks, model, step), BF16), pltpu.SemaphoreType.DMA((chunks,))]

    xs, bc, local, first, total, cumul = call(
        functools.partial(front_kernel, split),
        [
            ((length, width), BF16),
            ((length, 2 * states), BF16),
            ((states, width), F32),
            ((states + extra, width), BF16),
            ((8, width), F32),
            ((length, heads), F32),
        ],
        [in_hbm(tokens), in_hbm(decay), in_hbm(in_weight), in_hbm(qkv), in_hbm(attn_out)],
        3 * 10**9,
        [
            pltpu.VMEM(tokens.shape, BF16),
            pltpu.VMEM(decay.shape, F32),
            pltpu.VMEM((tall * row_split, lane_count), BF16),
            pltpu.VMEM((width // wide, model, wide), BF16),
            pltpu.VMEM((1, model, 2 * states), BF16),
            pltpu.SemaphoreType.DMA((4,)),
            pltpu.SemaphoreType.DMA((width // wide,)),
            pltpu.SemaphoreType.DMA((1,)),
        ],
        [HBM] * 5,
    )

    def link(sent, step):
        pairs = [(step, step + 1)]
        return lax.ppermute(sent, "seq", pairs)

    came = swap(first, "seq", 1)

    within, silu, grown, placing, cmat = call(
        middle_kernel,
        [
            ((length, width), F32),
            ((length, width), F32),
            ((length, width), F32),
            ((length, most), BF16),
            ((length, states), BF16),
        ],
        [tokens, decay, in_hbm(in_weight), cumul, xs, bc, groups],
        3 * 10**9,
        buffers,
        [VMEM, VMEM, HBM] + [VMEM] * 4,
    )

    kernel = functools.partial(first_merge_kernel, 0)
    outs = [((states, width), BF16)] * 2 + [((2 * tall, lane_count), BF16)]
    state, sent, bundle = call(kernel, outs, [came, first, total, local], 10**8)
    came = link(sent, 1)
    mask = 2
    while mask < devices:
        other = swap(bundle, "seq", mask)
        bundle = jnp.concatenate([bundle, other], axis=0)
        mask *= 2
    bundles, masks = [bundle], [0]
    for mask in range(2, lane_split * row_split, 2):
        bundles.append(swap(bundle, "grp", mask))
        masks.append(mask)
    if lane_split > 1:
        for i in range(len(bundles)):
            bundles.append(swap(bundles[i], "grp", 1))
            masks.append(masks[i] ^ 1)
    (weights,) = call(
        functools.partial(weight_kernel, masks, split, head_dim),
        [((4, devices * head_dim, model), BF16)],
        bundles,
        10**9,
    )

    kept, blocks, done = [], {}, 1
    bounds = stages(devices)
    for low, high in zip(bounds[:-1], bounds[1:]):
        while done < high - 1 and done < devices - 2:
            kernel = functools.partial(merge_kernel, done)
            ins = [came, state, total, local]
            state, sent = call(kernel, [((states, width), BF16)] * 2, ins, 10**8)
            done += 1
            came = link(sent, done)
        kept = call(
            functools.partial(post_kernel, low, high),
            [((length, model), BF16), ((most, model), BF16)],
            [came if high == devices else state, within, silu, grown, placing, cmat, gain]
            + [out_weight, tokens, inner]
            + list(kept),
            2 * 10**9,
        )
        if high < devices:
            for mask in range(1, devices):
                pairs = [(i, i ^ mask) for i in range(low, high) if i < i ^ mask]
                if pairs:
                    blocks.setdefault(mask, []).append(lax.ppermute(kept[1], "seq", pairs))

    inner_width = devices * head_dim
    sides = [((inner_width, most), BF16), ((most, inner_width), BF16)]
    query, key, value, bias = call(
        functools.partial(own_kernel, devices, length),
        [((most, inner_width), BF16)] + sides + [((most, devices * most), F32)],
        [kept[1], weights, groups],
        10**9,
    )
    keys, values = [key], [value]
    for mask in range(1, devices):
        key, value = call(project_kernel, sides, blocks[mask] + [weights], 5 * 10**8)
        keys.append(key)
        values.append(value)
    (result,) = call(
        functools.partial(attend_kernel, devices),
        [((length, model), BF16)],
        keys + values + [query, bias, weights, kept[0], placing],
        2 * 10**9,
    )
    return result


def stages(devices):
    return sorted({0, devices // 2, devices - 1, devices})


def solution(mesh):
    in_specs = (
        P(("grp", "seq"), None),
        P("grp"),
        P(("grp", "seq"), None),
        P(),
        P(),
        P(),
        P(),
        P("seq", None, None),
        P("seq", None, None),
    )
    out_specs = P(("grp", "seq"), None)
    return jax.shard_map(shards, mesh=mesh, in_specs=in_specs, out_specs=out_specs, check_vma=False)
```

```python
import functools

import jax
import jax.numpy as jnp
from jax import lax
from jax.experimental import pallas as pl
from jax.experimental.pallas import tpu as pltpu
from jax.sharding import PartitionSpec as P


F32 = jnp.float32
BF16 = jnp.bfloat16
EPS = 1e-05
VMEM = pl.BlockSpec(memory_space=pltpu.VMEM)
HBM = pl.BlockSpec(memory_space=pltpu.HBM)


def dot(a, b):
    return jnp.dot(a, b, preferred_element_type=F32)


def dot_rows(a, b):
    return lax.dot_general(a, b, (((0,), (0,)), ((), ())), preferred_element_type=F32)


def dot_lanes(a, b):
    return lax.dot_general(a, b, (((1,), (1,)), ((), ())), preferred_element_type=F32)


def iota(shape, axis):
    return lax.broadcasted_iota(jnp.int32, shape, axis)


def terms(value, count):
    out = []
    for _ in range(count):
        term = value.astype(BF16)
        out.append(term)
        value = value - term.astype(F32)
    return out


def spread(value, heads, width, count):
    size = width // heads
    row = lax.rem(iota((count * heads, width), 0), heads)
    lane = iota((count * heads, width), 1)
    pick = ((lane >= row * size) & (lane < (row + 1) * size)).astype(BF16)
    return dot(jnp.concatenate(terms(value, count), axis=1), pick)


def weight_copies(weight, buffer, sems, start, step):
    count = buffer.shape[0]
    return [
        pltpu.make_async_copy(
            weight.at[:, pl.ds(start + i * step, step)], buffer.at[i], sems.at[i]
        )
        for i in range(count)
    ]


def front_kernel(
    split, tokens_hbm, decay_hbm, weight, qkv, attn_out,
    xs, bc, local, first, total, cumul,
    tokens, decay, stack, xs_buffer, bc_buffer, small_sems, xs_sems, bc_sems,
):
    heads, length = decay.shape
    width = xs.shape[1]
    states = local.shape[0]
    step = xs_buffer.shape[2]
    bc_copy = weight_copies(weight, bc_buffer, bc_sems, 2 * width, 2 * states)
    xs_copy = weight_copies(weight, xs_buffer, xs_sems, 0, step)
    decay_copy = pltpu.make_async_copy(decay_hbm, decay, small_sems.at[0])
    token_copy = pltpu.make_async_copy(tokens_hbm, tokens, small_sems.at[1])
    mine = lax.rem(lax.axis_index("grp"), split[0] * split[1])
    lanes = stack.shape[1]
    column = pl.ds(pl.multiple_of(lax.rem(mine, split[0]) * lanes, lanes), lanes)
    upper_rows = qkv.shape[1]
    qkv_copy = pltpu.make_async_copy(
        qkv.at[0, :, column], stack.at[pl.ds(0, upper_rows)], small_sems.at[2]
    )
    out_copy = pltpu.make_async_copy(
        attn_out.at[0, :, column],
        stack.at[pl.ds(upper_rows, attn_out.shape[1])],
        small_sems.at[3],
    )
    for copy in [decay_copy, token_copy] + bc_copy + xs_copy + [qkv_copy, out_copy]:
        copy.start()

    decay_copy.wait()
    lower = (iota((length, length), 0) >= iota((length, length), 1)).astype(BF16)
    cum = sum(dot_lanes(lower, term) for term in terms(decay[...], 3))
    cumul[...] = cum
    last = cum[length - 1 :, :]
    tails = jnp.exp(last - cum)
    total[...] = spread(jnp.broadcast_to(jnp.exp(last), (8, heads)), heads, width, 3)
    tails_wide = spread(tails, heads, width, 2)

    token_copy.wait()
    bc_copy[0].wait()
    ins = tokens[...]
    both = dot(ins, bc_buffer[0]).astype(BF16)
    bc[...] = both
    for i, copy in enumerate(xs_copy):
        at = slice(i * step, (i + 1) * step)
        copy.wait()
        block = dot(ins, xs_buffer[i]).astype(BF16)
        xs[:, at] = block
        scaled = (block.astype(F32) * tails_wide[:, at]).astype(BF16)
        state = dot_rows(both, scaled)[:states]
        local[:, at] = state
        first[:states, at] = state.astype(BF16)

    qkv_copy.wait()
    out_copy.wait()
    tall = stack.shape[0] // split[1]
    part = lax.div(mine, split[0])
    piece = stack[pl.ds(pl.multiple_of(part * tall, tall), tall), :]
    few = first.shape[0] - states
    wide = stack.shape[1]
    for i in range(width // wide):
        first[states:, i * wide : (i + 1) * wide] = piece[i * few : (i + 1) * few]


def middle_kernel(
    tokens, decay, weight, cumul, xs, bc, groups,
    within, silu, grown, placing, cmat,
    gate_buffer, gate_sems,
):
    heads, length = decay.shape
    width = xs.shape[1]
    states = bc.shape[1] // 2
    step = gate_buffer.shape[2]
    most = placing.shape[1]
    copies = weight_copies(weight, gate_buffer, gate_sems, width, step)
    for copy in copies:
        copy.start()

    here = lax.axis_index("seq") * length
    count = groups.shape[1]
    position = here + iota((length, count), 0)
    group = jnp.broadcast_to(groups[...], (length, count))
    starts = jnp.sum((group == position).astype(F32), axis=1, keepdims=True)
    ahead = (group < position) & (group >= here)
    rank = jnp.sum(ahead.astype(F32), axis=1, keepdims=True).astype(jnp.int32)
    slot = iota((length, most), 1)
    placing[...] = jnp.where(slot == rank, starts, 0.0).astype(BF16)

    cum = cumul[...]
    upper = (iota((length, length), 0) <= iota((length, length), 1)).astype(BF16)
    cum_t = sum(dot(term, upper) for term in terms(decay[...], 3))
    grown[...] = spread(jnp.exp(cum), heads, width, 2)
    both = bc[...]
    cmat[...] = both[:, states:]
    mixed = dot_lanes(both[:, states:], both[:, :states])

    half = length // 2
    lower = iota((half, half), 0) >= iota((half, half), 1)
    size = width // heads
    pair = 2 * size
    left = iota((half, pair), 1) < size
    for at in range(0, heads, 2):
        lanes = slice(at * size, at * size + pair)
        early, late = xs[:half, lanes], xs[half:, lanes]
        tops, lows = [], []
        for head in (at, at + 1):
            column = cum[:, head : head + 1]
            row = cum_t[head : head + 1, :]
            apart = jnp.where(lower, column[:half] - row[:, :half], -jnp.inf)
            top = (jnp.exp(apart) * mixed[:half, :half]).astype(BF16)
            apart = jnp.where(lower, column[half:] - row[:, half:], -jnp.inf)
            low = (jnp.exp(apart) * mixed[half:, half:]).astype(BF16)
            across = jnp.exp(column[half:] - row[:, :half])
            across = (across * mixed[half:, :half]).astype(BF16)
            tops.append(dot(top, early))
            lows.append(dot(low, late) + dot(across, early))
        within[:half, lanes] = jnp.where(left, tops[0], tops[1])
        within[half:, lanes] = jnp.where(left, lows[0], lows[1])

    ins = tokens[...]
    for i, copy in enumerate(copies):
        copy.wait()
        gate = dot(ins, gate_buffer[i]).astype(BF16).astype(F32)
        silu[:, i * step : (i + 1) * step] = gate / (1.0 + jnp.exp(-gate))


def merge_kernel(step, came, before, total, local, state, sent):
    taken = lax.axis_index("seq") == step + 1
    value = jnp.where(taken, came[...].astype(F32), before[...].astype(F32))
    state[...] = value.astype(BF16)
    sent[...] = (total[0:1, :] * value + local[...]).astype(BF16)


def first_merge_kernel(step, came, first, total, local, state, sent, bundle):
    taken = lax.axis_index("seq") == step + 1
    states = local.shape[0]
    value = jnp.where(taken, came[:states, :].astype(F32), 0.0)
    state[...] = value.astype(BF16)
    sent[...] = (total[0:1, :] * value + local[...]).astype(BF16)
    few = came.shape[0] - states
    wide = bundle.shape[1]
    count = local.shape[1] // wide
    for j, source in enumerate((first, came)):
        for i in range(count):
            at = (j * count + i) * few
            bundle[at : at + few, :] = source[states:, i * wide : (i + 1) * wide]


def post_kernel(
    low, high, state, within, silu, grown, placing, cmat, gain, out_weight, tokens, inner_gain,
    *refs,
):
    earlier, (hidden, rows) = refs[:-2], refs[-2:]
    me = lax.axis_index("seq")
    active = (me >= low) & (me < high)

    @pl.when(active)
    def _():
        carried = dot(cmat[...], state[...])
        gated = (within[...] + grown[...] * carried) * silu[...]
        scale = lax.rsqrt(jnp.mean(gated * gated, axis=1, keepdims=True) + EPS)
        normed = (gated * scale * gain[...]).astype(BF16)
        mixed = dot(normed, out_weight[...])
        out = (tokens[...].astype(F32) + mixed).astype(BF16)
        hidden[...] = out
        picked = dot_rows(placing[...], out)
        scale = lax.rsqrt(jnp.mean(picked * picked, axis=1, keepdims=True) + EPS)
        rows[...] = (picked * scale * inner_gain[...]).astype(BF16)

    @pl.when(jnp.logical_not(active))
    def _():
        hidden[...] = earlier[0][...] if earlier else jnp.zeros_like(hidden)
        rows[...] = earlier[1][...] if earlier else jnp.zeros_like(rows)


def weight_kernel(masks, split, head_dim, *refs):
    bundles, out = refs[:-1], refs[-1]
    parts = out.shape[0] // split[1]
    lanes = bundles[0].shape[1]
    mine = lax.rem(lax.axis_index("grp"), split[0] * split[1])
    heads = out.shape[1] // head_dim
    for bundle, mask in zip(bundles, masks):
        source = mine ^ mask
        column = pl.ds(pl.multiple_of(lax.rem(source, split[0]) * lanes, lanes), lanes)
        part = lax.div(source, split[0]) * parts
        for head in range(heads):
            for j in range(parts):
                at = (head * parts + j) * head_dim
                out[part + j, head * head_dim : (head + 1) * head_dim, column] = bundle[
                    at : at + head_dim, :
                ]


def own_kernel(devices, length, rows, weights, groups, query, keys, values, bias):
    most = rows.shape[0]
    own = rows[...]
    query[...] = dot_lanes(own, weights[0]).astype(BF16)
    keys[...] = dot_lanes(weights[1], own).astype(BF16)
    values[...] = dot_lanes(own, weights[2]).astype(BF16)
    me = lax.axis_index("seq")
    slot = iota((most, most), 1)
    bias[:, :most] = jnp.where(slot <= iota((most, most), 0), 0.0, -jnp.inf)
    for back in range(1, devices):
        other = me ^ back
        start = other * length
        inside = (groups[...] >= start) & (groups[...] < start + length)
        count = jnp.sum(inside.astype(F32), axis=1, keepdims=True).astype(jnp.int32)
        seen = slot < jnp.where(other < me, count, 0)
        bias[:, back * most : (back + 1) * most] = jnp.where(seen, 0.0, -jnp.inf)


def project_kernel(mask, *refs):
    rows, (weights, keys, values) = refs[:-3], refs[-3:]
    me = lax.axis_index("seq")
    earlier = (me ^ mask) < me

    @pl.when(earlier)
    def _():
        block = sum(some[...] for some in rows)
        keys[...] = dot_lanes(weights[1], block).astype(BF16)
        values[...] = dot_lanes(block, weights[2]).astype(BF16)

    @pl.when(jnp.logical_not(earlier))
    def _():
        keys[...] = jnp.zeros_like(keys)
        values[...] = jnp.zeros_like(values)


def attend_kernel(devices, *refs):
    keys, refs = refs[:devices], refs[devices:]
    values, refs = refs[:devices], refs[devices:]
    query, bias, weights, hidden, placing, result = refs
    heads = devices
    head_dim = query.shape[1] // heads
    known = jnp.concatenate([block[...] for block in keys], axis=1)
    worth = jnp.concatenate([block[...] for block in values], axis=0)
    hide = bias[...]
    outs = []
    for head in range(heads):
        lanes = slice(head * head_dim, (head + 1) * head_dim)
        scores = dot(query[:, lanes], known[lanes, :]) * head_dim ** (-0.5) + hide
        top = jnp.max(scores, axis=1, keepdims=True)
        expo = jnp.exp(scores - top)
        share = 1.0 / jnp.sum(expo, axis=1, keepdims=True)
        outs.append(dot((expo * share).astype(BF16), worth[:, lanes]).astype(BF16))
    joined = jnp.concatenate(outs, axis=1)
    back = jnp.concatenate(terms(dot(joined, weights[3]), 2), axis=0)
    place = placing[...]
    placed = dot(jnp.concatenate([place, place], axis=1), back)
    result[...] = (hidden[...].astype(F32) + placed).astype(BF16)


def swap(value, axis, mask):
    pairs = [(i, i ^ mask) for i in range(lax.axis_size(axis))]
    return lax.ppermute(value, axis, pairs)


def in_hbm(value):
    return pltpu.with_memory_space_constraint(value, pltpu.HBM)


def call(kernel, outs, ins, cost, scratch=(), specs=None):
    kernel = pl.pallas_call(
        kernel,
        out_shape=[jax.ShapeDtypeStruct(shape, dtype) for shape, dtype in outs],
        in_specs=specs or [VMEM] * len(ins),
        out_specs=[VMEM] * len(outs),
        scratch_shapes=list(scratch),
        cost_estimate=pl.CostEstimate(flops=cost, transcendentals=0, bytes_accessed=0),
        compiler_params=pltpu.CompilerParams(vmem_limit_bytes=24 << 20),
    )
    return kernel(*ins)


def shards(
    tokens, group_pos, log_decay, in_weight, norm_gain, out_weight, inner_gain, qkv_weight, attn_out
):
    devices = lax.axis_size("seq")
    grps = lax.axis_size("grp")
    length, model = tokens.shape
    heads = log_decay.shape[1]
    width = out_weight.shape[0]
    states = (in_weight.shape[1] - 2 * width) // 2
    head_dim = attn_out.shape[1]
    most = length // 2
    lane_split = next(s for s in (4, 2, 1) if grps % s == 0 and model % (128 * s) == 0)
    row_split = 2 if grps % (2 * lane_split) == 0 else 1
    split = (lane_split, row_split)
    tall = 4 * head_dim // row_split
    lane_count = model // lane_split
    extra = tall * lane_count // width
    step = min(256, width)
    chunks = width // step
    wide = min(512, width)
    groups = group_pos.reshape(1, -1)
    decay = log_decay.T
    qkv = jnp.transpose(qkv_weight, (0, 2, 1))
    gain, inner = norm_gain.reshape(1, -1), inner_gain.reshape(1, -1)
    buffers = [pltpu.VMEM((chunks, model, step), BF16), pltpu.SemaphoreType.DMA((chunks,))]

    xs, bc, local, first, total, cumul = call(
        functools.partial(front_kernel, split),
        [
            ((length, width), BF16),
            ((length, 2 * states), BF16),
            ((states, width), F32),
            ((states + extra, width), BF16),
            ((8, width), F32),
            ((length, heads), F32),
        ],
        [in_hbm(tokens), in_hbm(decay), in_hbm(in_weight), in_hbm(qkv), in_hbm(attn_out)],
        3 * 10**9,
        [
            pltpu.VMEM(tokens.shape, BF16),
            pltpu.VMEM(decay.shape, F32),
            pltpu.VMEM((tall * row_split, lane_count), BF16),
            pltpu.VMEM((width // wide, model, wide), BF16),
            pltpu.VMEM((1, model, 2 * states), BF16),
            pltpu.SemaphoreType.DMA((4,)),
            pltpu.SemaphoreType.DMA((width // wide,)),
            pltpu.SemaphoreType.DMA((1,)),
        ],
        [HBM] * 5,
    )

    def link(sent, step):
        pairs = [(step, step + 1)]
        return lax.ppermute(sent, "seq", pairs)

    came = swap(first, "seq", 1)

    within, silu, grown, placing, cmat = call(
        middle_kernel,
        [
            ((length, width), F32),
            ((length, width), F32),
            ((length, width), F32),
            ((length, most), BF16),
            ((length, states), BF16),
        ],
        [tokens, decay, in_hbm(in_weight), cumul, xs, bc, groups],
        3 * 10**9,
        buffers,
        [VMEM, VMEM, HBM] + [VMEM] * 4,
    )

    kernel = functools.partial(first_merge_kernel, 0)
    outs = [((states, width), BF16)] * 2 + [((2 * tall, lane_count), BF16)]
    state, sent, bundle = call(kernel, outs, [came, first, total, local], 10**8)
    came = link(sent, 1)
    mask = 2
    while mask < devices:
        other = swap(bundle, "seq", mask)
        bundle = jnp.concatenate([bundle, other], axis=0)
        mask *= 2
    bundles, masks = [bundle], [0]
    for mask in range(2, lane_split * row_split, 2):
        bundles.append(swap(bundle, "grp", mask))
        masks.append(mask)
    if lane_split > 1:
        for i in range(len(bundles)):
            bundles.append(swap(bundles[i], "grp", 1))
            masks.append(masks[i] ^ 1)
    (weights,) = call(
        functools.partial(weight_kernel, masks, split, head_dim),
        [((4, devices * head_dim, model), BF16)],
        bundles,
        10**9,
    )

    kept, blocks, done = [], {}, 1
    bounds = stages(devices)
    for at, (low, high) in enumerate(zip(bounds[:-1], bounds[1:])):
        while done < high - 1 and done < devices - 2:
            kernel = functools.partial(merge_kernel, done)
            ins = [came, state, total, local]
            state, sent = call(kernel, [((states, width), BF16)] * 2, ins, 10**8)
            done += 1
            came = link(sent, done)
        kept = call(
            functools.partial(post_kernel, low, high),
            [((length, model), BF16), ((most, model), BF16)],
            [came if high == devices else state, within, silu, grown, placing, cmat, gain]
            + [out_weight, tokens, inner]
            + list(kept),
            2 * 10**9,
        )
        if high < devices:
            for mask in range(1, devices):
                far = mask >= devices // 2
                first_source = 0 if far and at == 1 else low
                pairs = [(i, i ^ mask) for i in range(first_source, high) if i < i ^ mask]
                if pairs and not (far and low == 0):
                    blocks.setdefault(mask, []).append(lax.ppermute(kept[1], "seq", pairs))

    inner_width = devices * head_dim
    sides = [((inner_width, most), BF16), ((most, inner_width), BF16)]
    query, key, value, bias = call(
        functools.partial(own_kernel, devices, length),
        [((most, inner_width), BF16)] + sides + [((most, devices * most), F32)],
        [kept[1], weights, groups],
        10**9,
    )
    keys, values = [key], [value]
    for mask in range(1, devices):
        kernel = functools.partial(project_kernel, mask)
        key, value = call(kernel, sides, blocks[mask] + [weights], 5 * 10**8)
        keys.append(key)
        values.append(value)
    (result,) = call(
        functools.partial(attend_kernel, devices),
        [((length, model), BF16)],
        keys + values + [query, bias, weights, kept[0], placing],
        2 * 10**9,
    )
    return result


def stages(devices):
    return sorted({0, 1, devices // 2, devices - 1, devices})


def solution(mesh):
    in_specs = (
        P(("grp", "seq"), None),
        P("grp"),
        P(("grp", "seq"), None),
        P(),
        P(),
        P(),
        P(),
        P("seq", None, None),
        P("seq", None, None),
    )
    out_specs = P(("grp", "seq"), None)
    return jax.shard_map(shards, mesh=mesh, in_specs=in_specs, out_specs=out_specs, check_vma=False)
```

```python
import functools
import math

import jax
import jax.numpy as jnp
from jax import lax
from jax.experimental import pallas as pl
from jax.experimental.pallas import tpu as pltpu
from jax.sharding import PartitionSpec as P


F32 = jnp.float32
BF16 = jnp.bfloat16
EPS = 1e-05
VMEM = pl.BlockSpec(memory_space=pltpu.VMEM)
HBM = pl.BlockSpec(memory_space=pltpu.HBM)


def dot(a, b):
    return jnp.dot(a, b, preferred_element_type=F32)


def dot_rows(a, b):
    return lax.dot_general(a, b, (((0,), (0,)), ((), ())), preferred_element_type=F32)


def dot_lanes(a, b):
    return lax.dot_general(a, b, (((1,), (1,)), ((), ())), preferred_element_type=F32)


def iota(shape, axis):
    return lax.broadcasted_iota(jnp.int32, shape, axis)


def terms(value, count):
    out = []
    for _ in range(count):
        term = value.astype(BF16)
        out.append(term)
        value = value - term.astype(F32)
    return out


def spread(value, heads, width, count):
    size = width // heads
    row = lax.rem(iota((count * heads, width), 0), heads)
    lane = iota((count * heads, width), 1)
    pick = ((lane >= row * size) & (lane < (row + 1) * size)).astype(BF16)
    return dot(jnp.concatenate(terms(value, count), axis=1), pick)


def weight_copies(weight, buffer, sems, start, step):
    count = buffer.shape[0]
    return [
        pltpu.make_async_copy(
            weight.at[:, pl.ds(start + i * step, step)], buffer.at[i], sems.at[i]
        )
        for i in range(count)
    ]


def front_kernel(
    split, tokens_hbm, decay_hbm, weight, qkv, attn_out,
    xs, bc, local, first, total, cumul,
    tokens, decay, stack, xs_buffer, bc_buffer, small_sems, xs_sems, bc_sems,
):
    heads, length = decay.shape
    width = xs.shape[1]
    states = local.shape[0]
    step = xs_buffer.shape[2]
    bc_copy = weight_copies(weight, bc_buffer, bc_sems, 2 * width, 2 * states)
    xs_copy = weight_copies(weight, xs_buffer, xs_sems, 0, step)
    decay_copy = pltpu.make_async_copy(decay_hbm, decay, small_sems.at[0])
    token_copy = pltpu.make_async_copy(tokens_hbm, tokens, small_sems.at[1])
    mine = lax.rem(lax.axis_index("grp"), split[0] * split[1])
    lanes = stack.shape[1]
    column = pl.ds(pl.multiple_of(lax.rem(mine, split[0]) * lanes, lanes), lanes)
    upper_rows = qkv.shape[1]
    qkv_copy = pltpu.make_async_copy(
        qkv.at[0, :, column], stack.at[pl.ds(0, upper_rows)], small_sems.at[2]
    )
    out_copy = pltpu.make_async_copy(
        attn_out.at[0, :, column],
        stack.at[pl.ds(upper_rows, attn_out.shape[1])],
        small_sems.at[3],
    )
    for copy in [decay_copy, token_copy] + bc_copy + xs_copy + [qkv_copy, out_copy]:
        copy.start()

    decay_copy.wait()
    lower = (iota((length, length), 0) >= iota((length, length), 1)).astype(BF16)
    cum = sum(dot_lanes(lower, term) for term in terms(decay[...], 3))
    cumul[...] = cum
    last = cum[length - 1 :, :]
    tails = jnp.exp(last - cum)
    total[...] = spread(jnp.broadcast_to(jnp.exp(last), (8, heads)), heads, width, 3)
    tails_wide = spread(tails, heads, width, 2)

    token_copy.wait()
    bc_copy[0].wait()
    ins = tokens[...]
    both = dot(ins, bc_buffer[0]).astype(BF16)
    bc[...] = both
    for i, copy in enumerate(xs_copy):
        at = slice(i * step, (i + 1) * step)
        copy.wait()
        block = dot(ins, xs_buffer[i]).astype(BF16)
        xs[:, at] = block
        scaled = (block.astype(F32) * tails_wide[:, at]).astype(BF16)
        state = dot_rows(both, scaled)[:states]
        local[:, at] = state
        first[:states, at] = state.astype(BF16)

    qkv_copy.wait()
    out_copy.wait()
    tall = stack.shape[0] // split[1]
    part = lax.div(mine, split[0])
    piece = stack[pl.ds(pl.multiple_of(part * tall, tall), tall), :]
    few = first.shape[0] - states
    wide = stack.shape[1]
    for i in range(width // wide):
        first[states:, i * wide : (i + 1) * wide] = piece[i * few : (i + 1) * few]


def middle_kernel(
    tokens, decay, weight, cumul, xs, bc, groups,
    within, silu, grown, placing, cmat,
    gate_buffer, gate_sems,
):
    heads, length = decay.shape
    width = xs.shape[1]
    states = bc.shape[1] // 2
    step = gate_buffer.shape[2]
    most = placing.shape[1]
    copies = weight_copies(weight, gate_buffer, gate_sems, width, step)
    for copy in copies:
        copy.start()

    here = lax.axis_index("seq") * length
    count = groups.shape[1]
    position = here + iota((length, count), 0)
    group = jnp.broadcast_to(groups[...], (length, count))
    starts = jnp.sum((group == position).astype(F32), axis=1, keepdims=True)
    ahead = (group < position) & (group >= here)
    rank = jnp.sum(ahead.astype(F32), axis=1, keepdims=True).astype(jnp.int32)
    slot = iota((length, most), 1)
    placing[...] = jnp.where(slot == rank, starts, 0.0).astype(BF16)

    cum = cumul[...]
    upper = (iota((length, length), 0) <= iota((length, length), 1)).astype(BF16)
    cum_t = sum(dot(term, upper) for term in terms(decay[...], 3))
    grown[...] = spread(jnp.exp(cum), heads, width, 2)
    both = bc[...]
    cmat[...] = both[:, states:]
    mixed = dot_lanes(both[:, states:], both[:, :states])

    half = length // 2
    lower = iota((half, half), 0) >= iota((half, half), 1)
    size = width // heads
    pair = 2 * size
    left = iota((half, pair), 1) < size
    for at in range(0, heads, 2):
        lanes = slice(at * size, at * size + pair)
        early, late = xs[:half, lanes], xs[half:, lanes]
        tops, lows = [], []
        for head in (at, at + 1):
            column = cum[:, head : head + 1]
            row = cum_t[head : head + 1, :]
            apart = jnp.where(lower, column[:half] - row[:, :half], -jnp.inf)
            top = (jnp.exp(apart) * mixed[:half, :half]).astype(BF16)
            apart = jnp.where(lower, column[half:] - row[:, half:], -jnp.inf)
            low = (jnp.exp(apart) * mixed[half:, half:]).astype(BF16)
            across = jnp.exp(column[half:] - row[:, :half])
            across = (across * mixed[half:, :half]).astype(BF16)
            tops.append(dot(top, early))
            lows.append(dot(low, late) + dot(across, early))
        within[:half, lanes] = jnp.where(left, tops[0], tops[1])
        within[half:, lanes] = jnp.where(left, lows[0], lows[1])

    ins = tokens[...]
    for i, copy in enumerate(copies):
        copy.wait()
        gate = dot(ins, gate_buffer[i]).astype(BF16).astype(F32)
        silu[:, i * step : (i + 1) * step] = gate / (1.0 + jnp.exp(-gate))


def merge_kernel(step, came, before, total, local, state, sent):
    taken = lax.axis_index("seq") == step + 1
    value = jnp.where(taken, came[...].astype(F32), before[...].astype(F32))
    state[...] = value.astype(BF16)
    sent[...] = (total[0:1, :] * value + local[...]).astype(BF16)


def first_merge_kernel(step, came, first, total, local, state, sent, bundle):
    taken = lax.axis_index("seq") == step + 1
    states = local.shape[0]
    value = jnp.where(taken, came[:states, :].astype(F32), 0.0)
    state[...] = value.astype(BF16)
    sent[...] = (total[0:1, :] * value + local[...]).astype(BF16)
    few = came.shape[0] - states
    wide = bundle.shape[1]
    count = local.shape[1] // wide
    for j, source in enumerate((first, came)):
        for i in range(count):
            at = (j * count + i) * few
            bundle[at : at + few, :] = source[states:, i * wide : (i + 1) * wide]


def post_kernel(
    low, high, state, within, silu, grown, placing, cmat, gain, out_weight, tokens, inner_gain,
    *refs,
):
    earlier, (hidden, rows) = refs[:-2], refs[-2:]
    me = lax.axis_index("seq")
    active = (me >= low) & (me < high)

    @pl.when(active)
    def _():
        carried = dot(cmat[...], state[...])
        gated = (within[...] + grown[...] * carried) * silu[...]
        scale = lax.rsqrt(jnp.mean(gated * gated, axis=1, keepdims=True) + EPS)
        normed = (gated * scale * gain[...]).astype(BF16)
        mixed = dot(normed, out_weight[...])
        out = (tokens[...].astype(F32) + mixed).astype(BF16)
        hidden[...] = out
        picked = dot_rows(placing[...], out)
        scale = lax.rsqrt(jnp.mean(picked * picked, axis=1, keepdims=True) + EPS)
        rows[...] = (picked * scale * inner_gain[...]).astype(BF16)

    @pl.when(jnp.logical_not(active))
    def _():
        hidden[...] = earlier[0][...] if earlier else jnp.zeros_like(hidden)
        rows[...] = earlier[1][...] if earlier else jnp.zeros_like(rows)


def weight_kernel(masks, split, head_dim, *refs):
    bundles, out = refs[:-1], refs[-1]
    parts = out.shape[0] // split[1]
    lanes = bundles[0].shape[1]
    mine = lax.rem(lax.axis_index("grp"), split[0] * split[1])
    heads = out.shape[1] // head_dim
    for bundle, mask in zip(bundles, masks):
        source = mine ^ mask
        column = pl.ds(pl.multiple_of(lax.rem(source, split[0]) * lanes, lanes), lanes)
        part = lax.div(source, split[0]) * parts
        for head in range(heads):
            for j in range(parts):
                at = (head * parts + j) * head_dim
                out[part + j, head * head_dim : (head + 1) * head_dim, column] = bundle[
                    at : at + head_dim, :
                ]


def exact_scale(size):
    return size ** (-0.5) == 2.0 ** round(math.log2(size ** (-0.5)))


def own_kernel(devices, length, rows, weights, groups, query, keys, values, bias):
    most = rows.shape[0]
    own = rows[...]
    size = weights.shape[1] // devices
    wanted = dot_lanes(own, weights[0]).astype(BF16).astype(F32)
    if exact_scale(size):
        wanted = wanted * size ** (-0.5)
    even = lax.rem(iota(wanted.shape, 1), 2 * size) < size
    query[0] = jnp.where(even, wanted, 0.0).astype(BF16)
    query[1] = jnp.where(even, 0.0, wanted).astype(BF16)
    keys[...] = dot_lanes(weights[1], own).astype(BF16)
    values[...] = dot_lanes(own, weights[2]).astype(BF16)
    me = lax.axis_index("seq")
    slot = iota((most, most), 1)
    bias[:, :most] = jnp.where(slot <= iota((most, most), 0), 0.0, -jnp.inf)
    for back in range(1, devices):
        other = me ^ back
        start = other * length
        inside = (groups[...] >= start) & (groups[...] < start + length)
        count = jnp.sum(inside.astype(F32), axis=1, keepdims=True).astype(jnp.int32)
        seen = slot < jnp.where(other < me, count, 0)
        bias[:, back * most : (back + 1) * most] = jnp.where(seen, 0.0, -jnp.inf)


def project_kernel(mask, *refs):
    rows, (weights, keys, values) = refs[:-3], refs[-3:]
    me = lax.axis_index("seq")
    earlier = (me ^ mask) < me

    @pl.when(earlier)
    def _():
        block = sum(some[...] for some in rows)
        keys[...] = dot_lanes(weights[1], block).astype(BF16)
        values[...] = dot_lanes(block, weights[2]).astype(BF16)

    @pl.when(jnp.logical_not(earlier))
    def _():
        keys[...] = jnp.zeros_like(keys)
        values[...] = jnp.zeros_like(values)


def attend_kernel(devices, *refs):
    keys, refs = refs[:devices], refs[devices:]
    values, refs = refs[:devices], refs[devices:]
    query, bias, weights, hidden, placing, result = refs
    most = query.shape[1]
    heads = devices
    size = query.shape[2] // heads
    known = jnp.concatenate([block[...] for block in keys], axis=1)
    worth = jnp.concatenate([block[...] for block in values], axis=0)
    hide = bias[...]
    left = iota((most, 2 * size), 1) < size
    outs = []
    for at in range(0, heads, 2):
        lanes = slice(at * size, (at + 2) * size)
        both = []
        for side in range(2):
            scores = dot(query[side, :, lanes], known[lanes, :])
            if not exact_scale(size):
                scores = scores * size ** (-0.5)
            scores = scores + hide
            top = jnp.max(scores, axis=1, keepdims=True)
            expo = jnp.exp(scores - top)
            share = 1.0 / jnp.sum(expo, axis=1, keepdims=True)
            both.append(dot((expo * share).astype(BF16), worth[:, lanes]))
        outs.append(jnp.where(left, both[0], both[1]).astype(BF16))
    joined = jnp.concatenate(outs, axis=1)
    back = jnp.concatenate(terms(dot(joined, weights[3]), 2), axis=0)
    place = placing[...]
    placed = dot(jnp.concatenate([place, place], axis=1), back)
    result[...] = (hidden[...].astype(F32) + placed).astype(BF16)


def swap(value, axis, mask):
    pairs = [(i, i ^ mask) for i in range(lax.axis_size(axis))]
    return lax.ppermute(value, axis, pairs)


def in_hbm(value):
    return pltpu.with_memory_space_constraint(value, pltpu.HBM)


def call(kernel, outs, ins, cost, scratch=(), specs=None):
    kernel = pl.pallas_call(
        kernel,
        out_shape=[jax.ShapeDtypeStruct(shape, dtype) for shape, dtype in outs],
        in_specs=specs or [VMEM] * len(ins),
        out_specs=[VMEM] * len(outs),
        scratch_shapes=list(scratch),
        cost_estimate=pl.CostEstimate(flops=cost, transcendentals=0, bytes_accessed=0),
        compiler_params=pltpu.CompilerParams(vmem_limit_bytes=24 << 20),
    )
    return kernel(*ins)


def shards(
    tokens, group_pos, log_decay, in_weight, norm_gain, out_weight, inner_gain, qkv_weight, attn_out
):
    devices = lax.axis_size("seq")
    grps = lax.axis_size("grp")
    length, model = tokens.shape
    heads = log_decay.shape[1]
    width = out_weight.shape[0]
    states = (in_weight.shape[1] - 2 * width) // 2
    head_dim = attn_out.shape[1]
    most = length // 2
    lane_split = next(s for s in (4, 2, 1) if grps % s == 0 and model % (128 * s) == 0)
    row_split = 2 if grps % (2 * lane_split) == 0 else 1
    split = (lane_split, row_split)
    tall = 4 * head_dim // row_split
    lane_count = model // lane_split
    extra = tall * lane_count // width
    step = min(256, width)
    chunks = width // step
    wide = min(512, width)
    groups = group_pos.reshape(1, -1)
    decay = log_decay.T
    qkv = jnp.transpose(qkv_weight, (0, 2, 1))
    gain, inner = norm_gain.reshape(1, -1), inner_gain.reshape(1, -1)
    buffers = [pltpu.VMEM((chunks, model, step), BF16), pltpu.SemaphoreType.DMA((chunks,))]

    xs, bc, local, first, total, cumul = call(
        functools.partial(front_kernel, split),
        [
            ((length, width), BF16),
            ((length, 2 * states), BF16),
            ((states, width), F32),
            ((states + extra, width), BF16),
            ((8, width), F32),
            ((length, heads), F32),
        ],
        [in_hbm(tokens), in_hbm(decay), in_hbm(in_weight), in_hbm(qkv), in_hbm(attn_out)],
        3 * 10**9,
        [
            pltpu.VMEM(tokens.shape, BF16),
            pltpu.VMEM(decay.shape, F32),
            pltpu.VMEM((tall * row_split, lane_count), BF16),
            pltpu.VMEM((width // wide, model, wide), BF16),
            pltpu.VMEM((1, model, 2 * states), BF16),
            pltpu.SemaphoreType.DMA((4,)),
            pltpu.SemaphoreType.DMA((width // wide,)),
            pltpu.SemaphoreType.DMA((1,)),
        ],
        [HBM] * 5,
    )

    def link(sent, step):
        pairs = [(step, step + 1)]
        return lax.ppermute(sent, "seq", pairs)

    came = swap(first, "seq", 1)

    within, silu, grown, placing, cmat = call(
        middle_kernel,
        [
            ((length, width), F32),
            ((length, width), F32),
            ((length, width), F32),
            ((length, most), BF16),
            ((length, states), BF16),
        ],
        [tokens, decay, in_hbm(in_weight), cumul, xs, bc, groups],
        3 * 10**9,
        buffers,
        [VMEM, VMEM, HBM] + [VMEM] * 4,
    )

    kernel = functools.partial(first_merge_kernel, 0)
    outs = [((states, width), BF16)] * 2 + [((2 * tall, lane_count), BF16)]
    state, sent, bundle = call(kernel, outs, [came, first, total, local], 10**8)
    came = link(sent, 1)
    mask = 2
    while mask < devices:
        other = swap(bundle, "seq", mask)
        bundle = jnp.concatenate([bundle, other], axis=0)
        mask *= 2
    bundles, masks = [bundle], [0]
    for mask in range(2, lane_split * row_split, 2):
        bundles.append(swap(bundle, "grp", mask))
        masks.append(mask)
    if lane_split > 1:
        for i in range(len(bundles)):
            bundles.append(swap(bundles[i], "grp", 1))
            masks.append(masks[i] ^ 1)
    (weights,) = call(
        functools.partial(weight_kernel, masks, split, head_dim),
        [((4, devices * head_dim, model), BF16)],
        bundles,
        10**9,
    )

    kept, blocks, done = [], {}, 1
    bounds = stages(devices)
    for at, (low, high) in enumerate(zip(bounds[:-1], bounds[1:])):
        while done < high - 1 and done < devices - 2:
            kernel = functools.partial(merge_kernel, done)
            ins = [came, state, total, local]
            state, sent = call(kernel, [((states, width), BF16)] * 2, ins, 10**8)
            done += 1
            came = link(sent, done)
        kept = call(
            functools.partial(post_kernel, low, high),
            [((length, model), BF16), ((most, model), BF16)],
            [came if high == devices else state, within, silu, grown, placing, cmat, gain]
            + [out_weight, tokens, inner]
            + list(kept),
            2 * 10**9,
        )
        if high < devices:
            for mask in range(1, devices):
                far = mask >= devices // 2
                first_source = 0 if far and at == 1 else low
                pairs = [(i, i ^ mask) for i in range(first_source, high) if i < i ^ mask]
                if pairs and not (far and low == 0):
                    blocks.setdefault(mask, []).append(lax.ppermute(kept[1], "seq", pairs))

    inner_width = devices * head_dim
    sides = [((inner_width, most), BF16), ((most, inner_width), BF16)]
    query, key, value, bias = call(
        functools.partial(own_kernel, devices, length),
        [((2, most, inner_width), BF16)] + sides + [((most, devices * most), F32)],
        [kept[1], weights, groups],
        10**9,
    )
    keys, values = [key], [value]
    for mask in range(1, devices):
        kernel = functools.partial(project_kernel, mask)
        key, value = call(kernel, sides, blocks[mask] + [weights], 5 * 10**8)
        keys.append(key)
        values.append(value)
    (result,) = call(
        functools.partial(attend_kernel, devices),
        [((length, model), BF16)],
        keys + values + [query, bias, weights, kept[0], placing],
        2 * 10**9,
    )
    return result


def stages(devices):
    return sorted({0, 1, devices // 2, devices - 1, devices})


def solution(mesh):
    in_specs = (
        P(("grp", "seq"), None),
        P("grp"),
        P(("grp", "seq"), None),
        P(),
        P(),
        P(),
        P(),
        P("seq", None, None),
        P("seq", None, None),
    )
    out_specs = P(("grp", "seq"), None)
    return jax.shard_map(shards, mesh=mesh, in_specs=in_specs, out_specs=out_specs, check_vma=False)
```
